32 devices in a mesh: parts: 2 (over x), row: 16 (over z, y, core).
Axes of the slice: x: 2, y: 2, z: 4, core: 2. Of those that a mesh axis runs over, the one named last changes fastest.
Arguments:
- raw_trace: float32 [320, 768, 512], P('row', 'parts'), parts along dimension 1, may hold values from -1200 to 1200
- fir_taps: float32 [32], replicated, may hold values from -1 to 1
- templ_real: bfloat16 [32, 320, 2048], P(None, None, 'row'), may hold values from -6 to 6
- templ_imag: bfloat16 [32, 320, 2048], P(None, None, 'row'), may hold values from -6 to 6
- channel_mask: int32 [320, 2048], P(None, 'row'), may hold values 0 or 1
- moveout: int32 [320, 2048], P(None, 'row'), may hold values from 0 to 63
Outputs:
- peak: float32 [2048, 768], P('row', 'parts'), parts along dimension 1
- best: float32 [768], P('parts'), parts along dimension 0
The draws below stay inside these ranges and needn't reach their ends.
There are 2 independent parts, one for each index of `parts`. The reference program is written for one: setup_inputs(seed, part) draws one part's arguments, and reference() takes and returns one part's arrays. A program takes and returns all parts, laid end to end along the dimension named above; an argument that names none is the same for every part. Nothing has to cross between parts.
All inputs are finite; a program needn't handle non-finite values. No bound on the sum of `channel_mask` on one device may be relied on, other than what follows from the above.
Results may differ from the reference program's by a relative error of at most 0.0015.
Values may be sent and summed in bfloat16 or wider, within the bound.
A program may use at most 128 MiB of HBM per device.

```python
import math
import jax
import jax.numpy as jnp
from jax import lax

CHANNELS = 320
SAMPLES = 256
BAND_BINS = 32
FIRST_BIN = 16
FILTER_TAPS = 32
MAX_MOVEOUT = 64
WINDOWS = 384
TEMPLATES = 2048


def draw_raw_trace(key, part):
    keys = jax.random.split(key, 3)
    ramp = 3.0 ** (jnp.arange(CHANNELS, dtype=jnp.float32) / max(CHANNELS - 1, 1))
    channel_gain = ramp * jnp.exp(jax.random.uniform(keys[0], (CHANNELS,), jnp.float32, 0.0, math.log(10.0)))
    window_gain = jnp.exp(jax.random.uniform(keys[1], (WINDOWS,), jnp.float32, 0.0, math.log(10.0)))
    shape = (CHANNELS, WINDOWS, 2 * SAMPLES)
    noise = jnp.clip(jax.random.normal(keys[2], shape, jnp.float32), -4.0, 4.0)
    return channel_gain[:, None, None] * window_gain[None, :, None] * noise


def set_ends(entries, rng, low, largest):
    place = [jax.random.randint(jax.random.fold_in(rng, axis), (), 0, length) for axis, length in enumerate(entries.shape)]
    widest = entries.shape.index(max(entries.shape))
    beside = place[:widest] + [(place[widest] + 1) % entries.shape[widest]] + place[widest + 1:]
    return entries.at[tuple(place)].set(low).at[tuple(beside)].set(largest)


def steps_of(key, extent, cuts, smallest, top_value):
    loudness, own = 1.0, jax.random.fold_in(key, 6)
    for axis_at, blocks in cuts:
        heights = jnp.exp(jax.random.uniform(jax.random.fold_in(own, axis_at), (blocks,), jnp.float32, smallest / len(cuts), top_value / len(cuts)))
        loudness = loudness * jnp.repeat(heights, extent[axis_at] // blocks).reshape([-1 if axis == axis_at else 1 for axis in range(len(extent))])
    return loudness


def normal_values(rng, extent, deviation, limit, cuts=(), kind=jnp.bfloat16):
    factor_of = steps_of(rng, extent, cuts, -0.22, 0.18) if cuts else 1.0
    result = jax.random.normal(rng, extent, jnp.float32) * deviation * factor_of
    return jnp.minimum(jnp.maximum(result, -limit), limit).astype(kind)


def setup_inputs(seed: int = 0, part: int = 0) -> dict:
    streams_of = jax.random.split(jax.random.key(seed), 7)
    part_splits = jax.random.split(jax.random.fold_in(streams_of[6], part), 7)
    return {
        "raw_trace": draw_raw_trace(jax.random.fold_in(jax.random.fold_in(streams_of[6], part), 71), part),
        "fir_taps": normal_values(streams_of[1], (FILTER_TAPS,), FILTER_TAPS ** -0.5, 1.0, (), jnp.float32),
        "templ_real": normal_values(streams_of[2], (BAND_BINS, CHANNELS, TEMPLATES), 1.0, 6.0, ((2, 16),)),
        "templ_imag": normal_values(streams_of[3], (BAND_BINS, CHANNELS, TEMPLATES), 1.0, 6.0, ((2, 16),)),
        "channel_mask": set_ends((jax.random.randint(streams_of[4], (CHANNELS, TEMPLATES), 0, 4) < 3).astype(jnp.int32), jax.random.fold_in(streams_of[4], 1), 0, 1),
        "moveout": set_ends(jax.random.randint(streams_of[5], (CHANNELS, TEMPLATES), 0, MAX_MOVEOUT), jax.random.fold_in(streams_of[5], 1), 0, MAX_MOVEOUT - 1).astype(jnp.int32),
    }


epsilon = 1e-06

def reference(raw_trace, fir_taps, templ_real, templ_imag, channel_mask, moveout):
    padded = jnp.pad(raw_trace, ((0, 0), (0, 0), (FILTER_TAPS - 1, 0)))
    decimated = jnp.zeros((CHANNELS, WINDOWS, SAMPLES), jnp.float32)
    for tap in range(FILTER_TAPS):
        begin = FILTER_TAPS - 1 - tap
        decimated = decimated + fir_taps[tap] * padded[:, :, begin:begin + 2 * SAMPLES:2]
    spectrum = jnp.fft.rfft(decimated, axis=-1)[:, :, FIRST_BIN:FIRST_BIN + BAND_BINS]
    spec_real = jnp.transpose(jnp.real(spectrum), (2, 0, 1)).astype(jnp.bfloat16)
    spec_imag = jnp.transpose(jnp.imag(spectrum), (2, 0, 1)).astype(jnp.bfloat16)
    real_wide = spec_real.astype(jnp.float32)
    imag_wide = spec_imag.astype(jnp.float32)
    energy = lax.optimization_barrier(jnp.sum(real_wide * real_wide + imag_wide * imag_wide, axis=(0, 1)))
    data_norm = jnp.sqrt(energy + epsilon)
    bin_index = FIRST_BIN + jnp.arange(BAND_BINS, dtype=jnp.int32)
    lag_index = jnp.arange(SAMPLES, dtype=jnp.int32)
    inverse_angle = 2.0 * math.pi / SAMPLES * (bin_index[:, None] * lag_index[None, :] % SAMPLES).astype(jnp.float32)
    inverse = jnp.concatenate([jnp.cos(inverse_angle), -jnp.sin(inverse_angle)], axis=0)
    scale = math.sqrt(2.0 * CHANNELS * BAND_BINS)
    block = math.gcd(TEMPLATES, 128)
    count = TEMPLATES // block

    def one_block(operands):
        real_block, imag_block, mask_block, shift_block = operands
        shift = bin_index[:, None, None] * shift_block[None, :, :] % SAMPLES
        phase = 2.0 * math.pi / SAMPLES * shift.astype(jnp.float32)
        cosine = jnp.cos(phase)
        sine = jnp.sin(phase)
        weight = mask_block.astype(jnp.float32)[None, :, :]
        real_in = real_block.astype(jnp.float32)
        imag_in = imag_block.astype(jnp.float32)
        eff_real = (weight * (real_in * cosine + imag_in * sine)).astype(jnp.bfloat16).astype(jnp.float32)
        eff_imag = (weight * (imag_in * cosine - real_in * sine)).astype(jnp.bfloat16).astype(jnp.float32)
        templ_norm = jnp.sqrt(lax.optimization_barrier(jnp.sum(eff_real * eff_real + eff_imag * eff_imag, axis=(0, 1))) + epsilon)
        cross_real = jnp.einsum('fct,fcw->ftw', eff_real, real_wide) + jnp.einsum('fct,fcw->ftw', eff_imag, imag_wide)
        cross_imag = jnp.einsum('fct,fcw->ftw', eff_real, imag_wide) - jnp.einsum('fct,fcw->ftw', eff_imag, real_wide)
        joined = jnp.concatenate([cross_real, cross_imag], axis=0)
        stacked = jnp.einsum('ftw,fn->twn', joined, inverse, precision=lax.Precision.HIGHEST)
        highest = lax.optimization_barrier(jnp.max(stacked, axis=2))
        return highest * scale / (templ_norm[:, None] * data_norm[None, :])
    real_blocks = jnp.transpose(templ_real.reshape(BAND_BINS, CHANNELS, count, block), (2, 0, 1, 3))
    imag_blocks = jnp.transpose(templ_imag.reshape(BAND_BINS, CHANNELS, count, block), (2, 0, 1, 3))
    mask_blocks = jnp.transpose(channel_mask.reshape(CHANNELS, count, block), (1, 0, 2))
    shift_blocks = jnp.transpose(moveout.reshape(CHANNELS, count, block), (1, 0, 2))
    peaks = lax.map(one_block, (real_blocks, imag_blocks, mask_blocks, shift_blocks))
    peak = peaks.reshape(TEMPLATES, WINDOWS)
    best = lax.optimization_barrier(jnp.max(peak, axis=0))
    return (peak, best)
```

```python
import functools
import math

import jax
import jax.numpy as jnp
import numpy as np
from jax import lax
from jax.experimental import pallas as pl
from jax.experimental.pallas import tpu as pltpu
from jax.sharding import PartitionSpec as P

FIRST_BIN = 16

epsilon = 1e-06
VMEM_LIMIT = 60 * 1024 * 1024


def front_kernel(taps_ref, forward_ref, raw_ref, out_ref, table, rows):
    local, block, length = raw_ref.shape
    samples = length // 2
    band2 = forward_ref.shape[1]
    band = band2 // 2

    @pl.when(pl.program_id(0) == 0)
    def _():
        offsets = 2 * lax.broadcasted_iota(jnp.int32, (length, samples), 1) - lax.broadcasted_iota(
            jnp.int32, (length, samples), 0
        )
        taps = jnp.zeros((length, samples), jnp.float32)
        for k in range(taps_ref.shape[0]):
            taps = jnp.where(offsets == k, taps_ref[k], taps)
        combined = jnp.dot(
            taps, forward_ref[...], precision=lax.Precision.HIGHEST, preferred_element_type=jnp.float32
        )
        high = combined.astype(jnp.bfloat16)
        low = (combined - high.astype(jnp.float32)).astype(jnp.bfloat16)
        table[...] = jnp.concatenate([high, low], axis=1)

    weights = table[...]
    for c in range(local):
        raw = raw_ref[c]
        high = raw.astype(jnp.bfloat16)
        low = (raw - high.astype(jnp.float32)).astype(jnp.bfloat16)
        spectra = jnp.dot(high, weights, preferred_element_type=jnp.float32) + jnp.dot(
            low, weights, preferred_element_type=jnp.float32
        )
        turned = spectra.T
        value = turned[:band2] + turned[band2:]
        rows[pl.ds(c, band, stride=2 * local), :] = value[:band]
        rows[pl.ds(local + c, band, stride=2 * local), :] = value[band:]
    out_ref[0] = rows[...].astype(jnp.bfloat16)


def template_kernel(x_ref, y_ref, cos_ref, sin_ref, cos1_ref, sin1_ref, out_ref, norm_ref, cosine, sine, total):
    f = pl.program_id(0)

    @pl.when(f == 0)
    def _():
        cosine[...] = cos_ref[...]
        sine[...] = sin_ref[...]
        total[...] = jnp.zeros_like(total)

    c, s = cosine[...], sine[...]
    x = x_ref[0].astype(jnp.float32)
    y = y_ref[0].astype(jnp.float32)
    first = (x * c + y * s).astype(jnp.bfloat16)
    second = (x * s - y * c).astype(jnp.bfloat16)
    back = first.astype(jnp.float32)
    square = back * back
    total[...] += jnp.sum(square.reshape(square.shape[0] // 8, 8, square.shape[1]), axis=0)
    out_ref[0] = jnp.concatenate([first, second], axis=1).T
    c1, s1 = cos1_ref[...], sin1_ref[...]
    cosine[...] = c * c1 - s * s1
    sine[...] = s * c1 + c * s1

    @pl.when(f == pl.num_programs(0) - 1)
    def _():
        norm_ref[...] = jnp.sum(total[...], axis=0, keepdims=True)


def scan_kernel(pitch, eff_ref, spec_ref, inverse_ref, high_ref, energy_ref, cross, total):
    step = pl.program_id(0)
    count = eff_ref.shape[0]
    band = pl.num_programs(0) * count
    templates = eff_ref.shape[1] // 2

    @pl.when(step == 0)
    def _():
        total[...] = jnp.zeros_like(total)

    for i in range(count):
        spec = spec_ref[i]
        wide = spec.astype(jnp.float32)
        square = wide * wide
        total[...] += jnp.sum(square.reshape(square.shape[0] // 8, 8, square.shape[1]), axis=0)
        both = jnp.dot(eff_ref[i], spec, preferred_element_type=jnp.float32)
        f = step * count + i
        cross[pl.ds(f, templates, stride=pitch), :] = both[:templates]
        cross[pl.ds(band + f, templates, stride=pitch), :] = both[templates:]

    @pl.when(step == pl.num_programs(0) - 1)
    def _():
        energy_ref[...] = jnp.sum(total[...], axis=0, keepdims=True)
        inverse = inverse_ref[...]

        def group(j, carry):
            found = []
            for k in range(0, 8, 2):
                pair = [
                    cross[pl.ds(pl.multiple_of((j * 8 + k + q) * pitch, 8), inverse.shape[1] // 3), :] for q in range(2)
                ]
                joined = jnp.concatenate(pair, axis=1)
                high = joined.astype(jnp.bfloat16)
                low = (joined - high.astype(jnp.float32)).astype(jnp.bfloat16)
                stacked = jnp.dot(
                    inverse,
                    jnp.concatenate([high, low, high], axis=0),
                    preferred_element_type=jnp.float32,
                )
                best = jnp.max(stacked, axis=0, keepdims=True)
                found += [best[:, : best.shape[1] // 2], best[:, best.shape[1] // 2 :]]
            high_ref[pl.ds(pl.multiple_of(j * 8, 8), 8), :] = jnp.concatenate(found, axis=0)
            return carry

        lax.fori_loop(0, templates // 8, group, 0)


def best_kernel(n, mine_ref, out_ref, slots, send_sem, recv_sem):
    me = lax.axis_index("row")
    barrier = pltpu.get_barrier_semaphore()
    for step in range(1, n):
        pl.semaphore_signal(
            barrier,
            inc=1,
            device_id={"row": lax.rem(me + step, n)},
            device_id_type=pl.DeviceIdType.MESH,
        )
    pl.semaphore_wait(barrier, n - 1)
    copies = []
    for step in range(1, n):
        copy = pltpu.make_async_remote_copy(
            src_ref=mine_ref,
            dst_ref=slots.at[step - 1],
            send_sem=send_sem.at[step - 1],
            recv_sem=recv_sem.at[step - 1],
            device_id={"row": lax.rem(me + step, n)},
            device_id_type=pl.DeviceIdType.MESH,
        )
        copy.start()
        copies.append(copy)
    value = mine_ref[...]
    for step in range(1, n):
        copies[step - 1].wait()
        value = jnp.maximum(value, slots[step - 1])
    out_ref[...] = value


def best_of_row(n, value):
    return pl.pallas_call(
        functools.partial(best_kernel, n),
        out_shape=jax.ShapeDtypeStruct(value.shape, value.dtype),
        in_specs=[pl.BlockSpec(memory_space=pltpu.VMEM)],
        out_specs=pl.BlockSpec(memory_space=pltpu.VMEM),
        scratch_shapes=[
            pltpu.VMEM((n - 1,) + value.shape, value.dtype),
            pltpu.SemaphoreType.DMA((n - 1,)),
            pltpu.SemaphoreType.DMA((n - 1,)),
        ],
        compiler_params=pltpu.CompilerParams(collective_id=0, has_side_effects=True),
        name="best_of_row",
    )(value)


def body(n, raw_trace, fir_taps, templ_real, templ_imag, channel_mask, moveout):
    local, windows, length = raw_trace.shape
    samples = length // 2
    band, channels, templates = templ_real.shape
    depth = 2 * channels
    block = math.gcd(windows, 128)
    blocks = windows // block
    bins = FIRST_BIN + np.arange(band)
    lags = np.arange(samples)
    angle = 2.0 * np.pi / samples * (bins[:, None] * lags[None, :] % samples)
    inverse = np.concatenate([np.cos(angle), -np.sin(angle)], axis=0)
    forward = jnp.asarray(inverse.T, jnp.float32)
    inverse = inverse.T.astype(np.float32)
    inverse_high = jnp.asarray(inverse).astype(jnp.bfloat16)
    high_np = np.asarray(inverse.astype(jnp.bfloat16))
    inverse_low = jnp.asarray((inverse - high_np.astype(np.float32)).astype(jnp.bfloat16))
    inverse3 = jnp.concatenate([inverse_high, inverse_high, inverse_low], axis=1)

    vmem = pl.BlockSpec(memory_space=pltpu.VMEM)
    spectra = pl.pallas_call(
        front_kernel,
        grid=(blocks,),
        out_shape=jax.ShapeDtypeStruct((blocks, band * 2 * local, block), jnp.bfloat16),
        in_specs=[
            pl.BlockSpec(memory_space=pltpu.SMEM),
            vmem,
            pl.BlockSpec((local, block, length), lambda i: (0, i, 0)),
        ],
        out_specs=pl.BlockSpec((1, band * 2 * local, block), lambda i: (i, 0, 0)),
        scratch_shapes=[
            pltpu.VMEM((length, 4 * band), jnp.bfloat16),
            pltpu.VMEM((band * 2 * local, block), jnp.float32),
        ],
        compiler_params=pltpu.CompilerParams(vmem_limit_bytes=VMEM_LIMIT),
        name="front",
    )(fir_taps, forward, raw_trace)
    spectra = spectra.reshape(blocks, band, 2 * local, block)
    gathered = [lax.all_gather(spectra[i], "row", axis=1, tiled=True) for i in range(blocks)]

    def rows_of(first, second):
        shape = first.shape[:-2] + (n, local, templates)
        joined = jnp.concatenate([first.reshape(shape), second.reshape(shape)], axis=-2)
        return joined.reshape(first.shape[:-2] + (depth, templates))

    x = rows_of(templ_real, templ_imag)
    y = rows_of(templ_imag, -templ_real)
    turn = 2.0 * math.pi / samples
    first_phase = turn * (FIRST_BIN * moveout % samples).astype(jnp.float32)
    step_phase = turn * moveout.astype(jnp.float32)
    weight = channel_mask.astype(jnp.float32)
    tables = [
        weight * jnp.cos(first_phase),
        weight * jnp.sin(first_phase),
        jnp.cos(step_phase),
        jnp.sin(step_phase),
    ]
    tables = [rows_of(table, table) for table in tables]
    one = pl.BlockSpec((1, depth, templates), lambda f: (f, 0, 0))
    eff, square = pl.pallas_call(
        template_kernel,
        grid=(band,),
        out_shape=(
            jax.ShapeDtypeStruct((band, 2 * templates, depth), jnp.bfloat16),
            jax.ShapeDtypeStruct((1, templates), jnp.float32),
        ),
        in_specs=[one, one, vmem, vmem, vmem, vmem],
        out_specs=(
            pl.BlockSpec((1, 2 * templates, depth), lambda f: (f, 0, 0)),
            pl.BlockSpec((1, templates), lambda f: (0, 0)),
        ),
        scratch_shapes=[
            pltpu.VMEM((depth, templates), jnp.float32),
            pltpu.VMEM((depth, templates), jnp.float32),
            pltpu.VMEM((8, templates), jnp.float32),
        ],
        compiler_params=pltpu.CompilerParams(vmem_limit_bytes=32 * 1024 * 1024),
        cost_estimate=pl.CostEstimate(flops=40 * band * depth * templates, bytes_accessed=8 * band * depth * templates, transcendentals=0),
        name="templates",
    )(x, y, *tables)

    count = math.gcd(band, 4)
    pitch = 2 * band + 8
    highest, energy = [], []
    for i in range(blocks):
        high, squares = pl.pallas_call(
            functools.partial(scan_kernel, pitch),
            grid=(band // count,),
            out_shape=(
                jax.ShapeDtypeStruct((templates, block), jnp.float32),
                jax.ShapeDtypeStruct((1, block), jnp.float32),
            ),
            in_specs=[
                pl.BlockSpec((count, 2 * templates, depth), lambda f: (f, 0, 0)),
                pl.BlockSpec((count, depth, block), lambda f: (f, 0, 0)),
                vmem,
            ],
            out_specs=(
                pl.BlockSpec((templates, block), lambda f: (0, 0)),
                pl.BlockSpec((1, block), lambda f: (0, 0)),
            ),
            scratch_shapes=[
                pltpu.VMEM((templates * pitch, block), jnp.float32),
                pltpu.VMEM((8, block), jnp.float32),
            ],
            compiler_params=pltpu.CompilerParams(vmem_limit_bytes=32 * 1024 * 1024),
            cost_estimate=pl.CostEstimate(flops=8 * band * depth * templates * block, bytes_accessed=16 * 1024 * 1024, transcendentals=0),
            name="scan",
        )(eff, gathered[i], inverse3)
        highest.append(high)
        energy.append(squares)
    highest = jnp.concatenate(highest, axis=1)
    data_norm = jnp.sqrt(jnp.concatenate(energy, axis=1) + epsilon)
    templ_norm = jnp.sqrt(square + epsilon).reshape(templates, 1)
    scale = math.sqrt(2.0 * channels * band)
    peak = highest * scale / (templ_norm * data_norm)
    best = best_of_row(n, jnp.max(peak, axis=0).reshape(blocks, block))
    return (peak, best.reshape(windows))


def solution(mesh):
    in_specs = (
        P("row", "parts", None),
        P(),
        P(None, None, "row"),
        P(None, None, "row"),
        P(None, "row"),
        P(None, "row"),
    )
    out_specs = (P("row", "parts"), P("parts"))
    return jax.shard_map(
        functools.partial(body, mesh.shape["row"]),
        mesh=mesh,
        in_specs=in_specs,
        out_specs=out_specs,
        check_vma=False,
    )
```

```python
import functools
import math

import jax
import jax.numpy as jnp
import numpy as np
from jax import lax
from jax.experimental import pallas as pl
from jax.experimental.pallas import tpu as pltpu
from jax.sharding import PartitionSpec as P

FIRST_BIN = 16

epsilon = 1e-06
VMEM_LIMIT = 60 * 1024 * 1024


def front_kernel(taps_ref, forward_ref, raw_ref, out_ref, table, rows):
    local, block, length = raw_ref.shape
    samples = length // 2
    band2 = forward_ref.shape[1]
    band = band2 // 2
    held = rows.shape[0] // band

    @pl.when(pl.program_id(0) == 0)
    def _():
        offsets = 2 * lax.broadcasted_iota(jnp.int32, (length, samples), 1) - lax.broadcasted_iota(
            jnp.int32, (length, samples), 0
        )
        taps = jnp.zeros((length, samples), jnp.float32)
        for k in range(taps_ref.shape[0]):
            taps = jnp.where(offsets == k, taps_ref[k], taps)
        combined = jnp.dot(
            taps, forward_ref[...], precision=lax.Precision.HIGHEST, preferred_element_type=jnp.float32
        )
        high = combined.astype(jnp.bfloat16)
        low = (combined - high.astype(jnp.float32)).astype(jnp.bfloat16)
        table[...] = jnp.concatenate([high, low], axis=1)
        if held > 2 * local:
            rows[...] = jnp.zeros_like(rows)

    weights = table[...]
    for c in range(local):
        raw = raw_ref[c]
        high = raw.astype(jnp.bfloat16)
        low = (raw - high.astype(jnp.float32)).astype(jnp.bfloat16)
        spectra = jnp.dot(high, weights, preferred_element_type=jnp.float32) + jnp.dot(
            low, weights, preferred_element_type=jnp.float32
        )
        turned = spectra.T
        value = turned[:band2] + turned[band2:]
        rows[pl.ds(c, band, stride=held), :] = value[:band]
        rows[pl.ds(local + c, band, stride=held), :] = value[band:]
    out_ref[0] = rows[...].astype(jnp.bfloat16)


def template_kernel(x_ref, y_ref, cos_ref, sin_ref, cos1_ref, sin1_ref, out_ref, norm_ref, cosine, sine, total):
    f = pl.program_id(0)

    @pl.when(f == 0)
    def _():
        cosine[...] = cos_ref[...]
        sine[...] = sin_ref[...]
        total[...] = jnp.zeros_like(total)

    c, s = cosine[...], sine[...]
    x = x_ref[0].astype(jnp.float32)
    y = y_ref[0].astype(jnp.float32)
    first = (x * c + y * s).astype(jnp.bfloat16)
    second = (x * s - y * c).astype(jnp.bfloat16)
    back = first.astype(jnp.float32)
    square = back * back
    total[...] += jnp.sum(square.reshape(square.shape[0] // 8, 8, square.shape[1]), axis=0)
    out_ref[0] = jnp.concatenate([first, second], axis=1).T
    c1, s1 = cos1_ref[...], sin1_ref[...]
    cosine[...] = c * c1 - s * s1
    sine[...] = s * c1 + c * s1

    @pl.when(f == pl.num_programs(0) - 1)
    def _():
        norm_ref[...] = jnp.sum(total[...], axis=0, keepdims=True)


def scan_kernel(n, pitch, count, eff_ref, inverse_ref, spec_ref, high_ref, energy_ref, gathered, buffer, cross, total, send_sem, recv_sem, own_sem, load_sem):
    blocks, band, held, block = spec_ref.shape
    templates = eff_ref.shape[1] // 2
    layers = n // 4
    me = lax.axis_index("row")
    z, y, core = me // 4, lax.rem(me // 2, 2), lax.rem(me, 2)

    def index(z, y, core):
        return z * 4 + y * 2 + core

    def place(i, origin):
        return gathered.at[i, :, pl.ds(pl.multiple_of(origin * held, 8), held), :]

    def send(i, origin, target, kind, own=False):
        return pltpu.make_async_remote_copy(
            src_ref=spec_ref.at[i] if own else place(i, origin),
            dst_ref=place(i, origin),
            send_sem=send_sem.at[kind, i],
            recv_sem=recv_sem.at[i, origin],
            device_id={"row": target},
            device_id_type=pl.DeviceIdType.MESH,
        )

    def arrived(i, origin):
        send(i, origin, index(z, y, 1 - core), 0).wait_recv()

    across = index(z, 1 - y, core)
    partner = index(z, y, 1 - core)
    barrier = pltpu.get_barrier_semaphore()
    targets = [index(lax.rem(z + s, layers), y, core) for s in range(1, layers)]
    for target in targets + [across, partner]:
        pl.semaphore_signal(barrier, inc=1, device_id={"row": target}, device_id_type=pl.DeviceIdType.MESH)
    pl.semaphore_wait(barrier, layers + 1)

    sends = []

    def start(i, origin, target, kind, own=False):
        copy = send(i, origin, target, kind, own)
        copy.start()
        sends.append(copy)

    own = [pltpu.make_async_copy(spec_ref.at[i], place(i, me), own_sem.at[i]) for i in range(blocks)]
    for i in range(blocks):
        start(i, me, across, 0, True)
        for s in range(1, layers):
            start(i, me, targets[s - 1], 2 * n + s, True)
        start(i, me, partner, n, True)
        own[i].start()

    def along(i):
        for s in range(1, layers):
            origin = index(lax.rem(z + s, layers), y, core)
            arrived(i, origin)
            start(i, origin, across, s, False)
            start(i, origin, partner, n + s, False)

    def over(i):
        for s in range(layers):
            origin = index(lax.rem(z + s, layers), 1 - y, core)
            arrived(i, origin)
            start(i, origin, partner, n + layers + s, False)

    def beside(i):
        for s in range(layers):
            for side in (y, 1 - y):
                arrived(i, index(lax.rem(z + s, layers), side, 1 - core))

    inverse = inverse_ref[...]

    def scan(i):
        own[i].wait()
        loads = [
            pltpu.make_async_copy(
                gathered.at[i, pl.ds(g * count, count)], buffer.at[pl.ds(g * count, count)], load_sem.at[g]
            )
            for g in range(band // count)
        ]
        for load in loads:
            load.start()
        total[...] = jnp.zeros_like(total)
        for g, load in enumerate(loads):
            load.wait()

            def one(f, carry):
                spec = buffer[f]
                wide = spec.astype(jnp.float32)
                square = wide * wide
                total[...] += jnp.sum(square.reshape(square.shape[0] // 8, 8, square.shape[1]), axis=0)
                both = jnp.dot(eff_ref[f], spec, preferred_element_type=jnp.float32)
                cross[pl.ds(f, templates, stride=pitch), :] = both[:templates]
                cross[pl.ds(band + f, templates, stride=pitch), :] = both[templates:]
                return carry

            lax.fori_loop(g * count, (g + 1) * count, one, 0)
        energy_ref[i] = jnp.sum(total[...], axis=0, keepdims=True)

        def group(j, carry):
            found = []
            for k in range(0, 8, 2):
                pair = [
                    cross[pl.ds(pl.multiple_of((j * 8 + k + q) * pitch, 8), 2 * band), :] for q in range(2)
                ]
                joined = jnp.concatenate(pair, axis=1)
                high = joined.astype(jnp.bfloat16)
                low = (joined - high.astype(jnp.float32)).astype(jnp.bfloat16)
                stacked = jnp.dot(
                    inverse,
                    jnp.concatenate([high, low, high], axis=0),
                    preferred_element_type=jnp.float32,
                )
                best = jnp.max(stacked, axis=0, keepdims=True)
                found += [best[:, :block], best[:, block:]]
            high_ref[pl.ds(pl.multiple_of(j * 8, 8), 8), i * block : (i + 1) * block] = jnp.concatenate(found, axis=0)
            return carry

        lax.fori_loop(0, templates // 8, group, 0)

    along(0)
    over(0)
    for i in range(blocks):
        if i + 1 < blocks:
            along(i + 1)
        beside(i)
        scan(i)
        if i + 1 < blocks:
            over(i + 1)
    for copy in sends:
        copy.wait_send()


def best_kernel(n, mine_ref, out_ref, slots, send_sem, recv_sem):
    me = lax.axis_index("row")
    barrier = pltpu.get_barrier_semaphore()
    for step in range(1, n):
        pl.semaphore_signal(
            barrier,
            inc=1,
            device_id={"row": lax.rem(me + step, n)},
            device_id_type=pl.DeviceIdType.MESH,
        )
    pl.semaphore_wait(barrier, n - 1)
    copies = []
    for step in range(1, n):
        copy = pltpu.make_async_remote_copy(
            src_ref=mine_ref,
            dst_ref=slots.at[step - 1],
            send_sem=send_sem.at[step - 1],
            recv_sem=recv_sem.at[step - 1],
            device_id={"row": lax.rem(me + step, n)},
            device_id_type=pl.DeviceIdType.MESH,
        )
        copy.start()
        copies.append(copy)
    value = mine_ref[...]
    for step in range(1, n):
        copies[step - 1].wait()
        value = jnp.maximum(value, slots[step - 1])
    out_ref[...] = value


def best_of_row(n, value):
    return pl.pallas_call(
        functools.partial(best_kernel, n),
        out_shape=jax.ShapeDtypeStruct(value.shape, value.dtype),
        in_specs=[pl.BlockSpec(memory_space=pltpu.VMEM)],
        out_specs=pl.BlockSpec(memory_space=pltpu.VMEM),
        scratch_shapes=[
            pltpu.VMEM((n - 1,) + value.shape, value.dtype),
            pltpu.SemaphoreType.DMA((n - 1,)),
            pltpu.SemaphoreType.DMA((n - 1,)),
        ],
        compiler_params=pltpu.CompilerParams(collective_id=0, has_side_effects=True),
        name="best_of_row",
    )(value)


def body(n, raw_trace, fir_taps, templ_real, templ_imag, channel_mask, moveout):
    local, windows, length = raw_trace.shape
    samples = length // 2
    band, channels, templates = templ_real.shape
    held = -(-2 * local // 8) * 8
    depth = n * held
    block = math.gcd(windows, 128)
    blocks = windows // block
    bins = FIRST_BIN + np.arange(band)
    lags = np.arange(samples)
    angle = 2.0 * np.pi / samples * (bins[:, None] * lags[None, :] % samples)
    inverse = np.concatenate([np.cos(angle), -np.sin(angle)], axis=0)
    forward = jnp.asarray(inverse.T, jnp.float32)
    inverse = inverse.T.astype(np.float32)
    inverse_high = jnp.asarray(inverse).astype(jnp.bfloat16)
    high_np = np.asarray(inverse.astype(jnp.bfloat16))
    inverse_low = jnp.asarray((inverse - high_np.astype(np.float32)).astype(jnp.bfloat16))
    inverse3 = jnp.concatenate([inverse_high, inverse_high, inverse_low], axis=1)

    vmem = pl.BlockSpec(memory_space=pltpu.VMEM)
    spectra = pl.pallas_call(
        front_kernel,
        grid=(blocks,),
        out_shape=jax.ShapeDtypeStruct((blocks, band * held, block), jnp.bfloat16),
        in_specs=[
            pl.BlockSpec(memory_space=pltpu.SMEM),
            vmem,
            pl.BlockSpec((local, block, length), lambda i: (0, i, 0)),
        ],
        out_specs=pl.BlockSpec((1, band * held, block), lambda i: (i, 0, 0)),
        scratch_shapes=[
            pltpu.VMEM((length, 4 * band), jnp.bfloat16),
            pltpu.VMEM((band * held, block), jnp.float32),
        ],
        compiler_params=pltpu.CompilerParams(vmem_limit_bytes=VMEM_LIMIT),
        name="front",
    )(fir_taps, forward, raw_trace)
    spectra = spectra.reshape(blocks, band, held, block)

    def rows_of(first, second):
        shape = first.shape[:-2] + (n, local, templates)
        joined = jnp.concatenate([first.reshape(shape), second.reshape(shape)], axis=-2)
        if held > 2 * local:
            joined = jnp.pad(joined, [(0, 0)] * (joined.ndim - 2) + [(0, held - 2 * local), (0, 0)])
        return joined.reshape(first.shape[:-2] + (depth, templates))

    x = rows_of(templ_real, templ_imag)
    y = rows_of(templ_imag, -templ_real)
    turn = 2.0 * math.pi / samples
    first_phase = turn * (FIRST_BIN * moveout % samples).astype(jnp.float32)
    step_phase = turn * moveout.astype(jnp.float32)
    weight = channel_mask.astype(jnp.float32)
    tables = [
        weight * jnp.cos(first_phase),
        weight * jnp.sin(first_phase),
        jnp.cos(step_phase),
        jnp.sin(step_phase),
    ]
    tables = [rows_of(table, table) for table in tables]
    one = pl.BlockSpec((1, depth, templates), lambda f: (f, 0, 0))
    eff, square = pl.pallas_call(
        template_kernel,
        grid=(band,),
        out_shape=(
            jax.ShapeDtypeStruct((band, 2 * templates, depth), jnp.bfloat16),
            jax.ShapeDtypeStruct((1, templates), jnp.float32),
        ),
        in_specs=[one, one, vmem, vmem, vmem, vmem],
        out_specs=(
            pl.BlockSpec((1, 2 * templates, depth), lambda f: (f, 0, 0)),
            pl.BlockSpec((1, templates), lambda f: (0, 0)),
        ),
        scratch_shapes=[
            pltpu.VMEM((depth, templates), jnp.float32),
            pltpu.VMEM((depth, templates), jnp.float32),
            pltpu.VMEM((8, templates), jnp.float32),
        ],
        compiler_params=pltpu.CompilerParams(vmem_limit_bytes=32 * 1024 * 1024),
        cost_estimate=pl.CostEstimate(flops=40 * band * depth * templates, bytes_accessed=8 * band * depth * templates, transcendentals=0),
        name="templates",
    )(x, y, *tables)

    count = math.gcd(band, 4)
    pitch = 2 * band + 8
    anywhere = pl.BlockSpec(memory_space=pl.ANY)
    highest, energy, _ = pl.pallas_call(
        functools.partial(scan_kernel, n, pitch, count),
        out_shape=(
            jax.ShapeDtypeStruct((templates, windows), jnp.float32),
            jax.ShapeDtypeStruct((blocks, 1, block), jnp.float32),
            jax.ShapeDtypeStruct((blocks, band, depth, block), jnp.bfloat16),
        ),
        in_specs=[vmem, vmem, anywhere],
        out_specs=(vmem, vmem, anywhere),
        scratch_shapes=[
            pltpu.VMEM((band, depth, block), jnp.bfloat16),
            pltpu.VMEM((templates * pitch, block), jnp.float32),
            pltpu.VMEM((8, block), jnp.float32),
            pltpu.SemaphoreType.DMA((3 * n, blocks)),
            pltpu.SemaphoreType.DMA((blocks, n)),
            pltpu.SemaphoreType.DMA((blocks,)),
            pltpu.SemaphoreType.DMA((band // count,)),
        ],
        compiler_params=pltpu.CompilerParams(
            collective_id=1, has_side_effects=True, vmem_limit_bytes=VMEM_LIMIT
        ),
        name="gather_scan",
    )(eff, inverse3, spectra)
    data_norm = jnp.sqrt(energy.reshape(1, windows) + epsilon)
    templ_norm = jnp.sqrt(square + epsilon).reshape(templates, 1)
    scale = math.sqrt(2.0 * channels * band)
    peak = highest * scale / (templ_norm * data_norm)
    best = best_of_row(n, jnp.max(peak, axis=0).reshape(blocks, block))
    return (peak, best.reshape(windows))


def solution(mesh):
    in_specs = (
        P("row", "parts", None),
        P(),
        P(None, None, "row"),
        P(None, None, "row"),
        P(None, "row"),
        P(None, "row"),
    )
    out_specs = (P("row", "parts"), P("parts"))
    return jax.shard_map(
        functools.partial(body, mesh.shape["row"]),
        mesh=mesh,
        in_specs=in_specs,
        out_specs=out_specs,
        check_vma=False,
    )
```

```python
import functools
import math

import jax
import jax.numpy as jnp
import numpy as np
from jax import lax
from jax.experimental import pallas as pl
from jax.experimental.pallas import tpu as pltpu
from jax.sharding import PartitionSpec as P

FIRST_BIN = 16

epsilon = 1e-06
VMEM_LIMIT = 60 * 1024 * 1024


def front_kernel(taps_ref, forward_ref, raw_ref, out_ref, table, rows):
    local, block, length = raw_ref.shape
    samples = length // 2
    band2 = forward_ref.shape[1]
    band = band2 // 2
    held = rows.shape[0] // band

    @pl.when(pl.program_id(0) == 0)
    def _():
        offsets = 2 * lax.broadcasted_iota(jnp.int32, (length, samples), 1) - lax.broadcasted_iota(
            jnp.int32, (length, samples), 0
        )
        taps = jnp.zeros((length, samples), jnp.float32)
        for k in range(taps_ref.shape[0]):
            taps = jnp.where(offsets == k, taps_ref[k], taps)
        combined = jnp.dot(
            taps, forward_ref[...], precision=lax.Precision.HIGHEST, preferred_element_type=jnp.float32
        )
        high = combined.astype(jnp.bfloat16)
        low = (combined - high.astype(jnp.float32)).astype(jnp.bfloat16)
        table[...] = jnp.concatenate([high, low], axis=1)
        if held > 2 * local:
            rows[...] = jnp.zeros_like(rows)

    weights = table[...]
    for c in range(local):
        raw = raw_ref[c]
        high = raw.astype(jnp.bfloat16)
        low = (raw - high.astype(jnp.float32)).astype(jnp.bfloat16)
        spectra = jnp.dot(high, weights, preferred_element_type=jnp.float32) + jnp.dot(
            low, weights, preferred_element_type=jnp.float32
        )
        turned = spectra.T
        value = turned[:band2] + turned[band2:]
        rows[pl.ds(c, band, stride=held), :] = value[:band]
        rows[pl.ds(local + c, band, stride=held), :] = value[band:]
    out_ref[0] = rows[...].astype(jnp.bfloat16)


def scan_kernel(n, pitch, count, x_ref, y_ref, cos_ref, sin_ref, cos1_ref, sin1_ref, inverse_ref, spec_ref, high_ref, energy_ref, norm_ref, gathered, eff_ref, cosine, sine, buffer, cross, total, send_sem, recv_sem, own_sem, load_sem):
    blocks, band, held, block = spec_ref.shape
    templates = x_ref.shape[2]
    layers = n // 4
    me = lax.axis_index("row")
    z, y, core = me // 4, lax.rem(me // 2, 2), lax.rem(me, 2)

    def index(z, y, core):
        return z * 4 + y * 2 + core

    def place(i, origin):
        return gathered.at[i, :, pl.ds(pl.multiple_of(origin * held, 8), held), :]

    def send(i, origin, target, kind, own=False):
        return pltpu.make_async_remote_copy(
            src_ref=spec_ref.at[i] if own else place(i, origin),
            dst_ref=place(i, origin),
            send_sem=send_sem.at[kind, i],
            recv_sem=recv_sem.at[i, origin],
            device_id={"row": target},
            device_id_type=pl.DeviceIdType.MESH,
        )

    def arrived(i, origin):
        send(i, origin, index(z, y, 1 - core), 0).wait_recv()

    across = index(z, 1 - y, core)
    partner = index(z, y, 1 - core)
    barrier = pltpu.get_barrier_semaphore()
    targets = [index(lax.rem(z + s, layers), y, core) for s in range(1, layers)]
    for target in targets + [across, partner]:
        pl.semaphore_signal(barrier, inc=1, device_id={"row": target}, device_id_type=pl.DeviceIdType.MESH)
    pl.semaphore_wait(barrier, layers + 1)

    sends = []

    def start(i, origin, target, kind, own=False):
        copy = send(i, origin, target, kind, own)
        copy.start()
        sends.append(copy)

    own = [pltpu.make_async_copy(spec_ref.at[i], place(i, me), own_sem.at[i]) for i in range(blocks)]
    for i in range(blocks):
        start(i, me, across, 0, True)
        for s in range(1, layers):
            start(i, me, targets[s - 1], 2 * n + s, True)
        start(i, me, partner, n, True)
        own[i].start()

    def along(i):
        for s in range(1, layers):
            origin = index(lax.rem(z + s, layers), y, core)
            arrived(i, origin)
            start(i, origin, across, s, False)
            start(i, origin, partner, n + s, False)

    def over(i):
        for s in range(layers):
            origin = index(lax.rem(z + s, layers), 1 - y, core)
            arrived(i, origin)
            start(i, origin, partner, n + layers + s, False)

    def beside(i):
        for s in range(layers):
            for side in (y, 1 - y):
                arrived(i, index(lax.rem(z + s, layers), side, 1 - core))

    inverse = inverse_ref[...]

    def scan(i):
        own[i].wait()
        loads = [
            pltpu.make_async_copy(
                gathered.at[i, pl.ds(g * count, count)], buffer.at[pl.ds(g * count, count)], load_sem.at[g]
            )
            for g in range(band // count)
        ]
        for load in loads:
            load.start()
        total[...] = jnp.zeros_like(total)
        for g, load in enumerate(loads):
            load.wait()

            def one(f, carry):
                spec = buffer[f]
                wide = spec.astype(jnp.float32)
                square = wide * wide
                total[:, :block] += jnp.sum(square.reshape(square.shape[0] // 8, 8, square.shape[1]), axis=0)
                both = jnp.dot(eff_ref[f], spec, preferred_element_type=jnp.float32)
                cross[pl.ds(f, templates, stride=pitch), :] = both[:templates]
                cross[pl.ds(band + f, templates, stride=pitch), :] = both[templates:]
                return carry

            lax.fori_loop(g * count, (g + 1) * count, one, 0)
        energy_ref[i] = jnp.sum(total[:, :block], axis=0, keepdims=True)

        def group(j, carry):
            found = []
            for k in range(0, 8, 2):
                pair = [
                    cross[pl.ds(pl.multiple_of((j * 8 + k + q) * pitch, 8), 2 * band), :] for q in range(2)
                ]
                joined = jnp.concatenate(pair, axis=1)
                high = joined.astype(jnp.bfloat16)
                low = (joined - high.astype(jnp.float32)).astype(jnp.bfloat16)
                stacked = jnp.dot(
                    inverse,
                    jnp.concatenate([high, low, high], axis=0),
                    preferred_element_type=jnp.float32,
                )
                best = jnp.max(stacked, axis=0, keepdims=True)
                found += [best[:, :block], best[:, block:]]
            high_ref[pl.ds(pl.multiple_of(j * 8, 8), 8), i * block : (i + 1) * block] = jnp.concatenate(found, axis=0)
            return carry

        lax.fori_loop(0, templates // 8, group, 0)

    cosine[...] = cos_ref[...]
    sine[...] = sin_ref[...]
    total[...] = jnp.zeros_like(total)

    def prepare(f, carry):
        c, s = cosine[...], sine[...]
        x = x_ref[f].astype(jnp.float32)
        y = y_ref[f].astype(jnp.float32)
        first = (x * c + y * s).astype(jnp.bfloat16)
        second = (x * s - y * c).astype(jnp.bfloat16)
        back = first.astype(jnp.float32)
        square = back * back
        total[:, :templates] += jnp.sum(square.reshape(square.shape[0] // 8, 8, templates), axis=0)
        eff_ref[f] = jnp.concatenate([first, second], axis=1).T
        c1, s1 = cos1_ref[...], sin1_ref[...]
        cosine[...] = c * c1 - s * s1
        sine[...] = s * c1 + c * s1
        return carry

    lax.fori_loop(0, band, prepare, 0)
    norm_ref[...] = jnp.sum(total[:, :templates], axis=0, keepdims=True)

    along(0)
    over(0)
    for i in range(blocks):
        if i + 1 < blocks:
            along(i + 1)
        beside(i)
        scan(i)
        if i + 1 < blocks:
            over(i + 1)
    for copy in sends:
        copy.wait_send()


def best_kernel(n, mine_ref, out_ref, slots, send_sem, recv_sem):
    me = lax.axis_index("row")
    barrier = pltpu.get_barrier_semaphore()
    for step in range(1, n):
        pl.semaphore_signal(
            barrier,
            inc=1,
            device_id={"row": lax.rem(me + step, n)},
            device_id_type=pl.DeviceIdType.MESH,
        )
    pl.semaphore_wait(barrier, n - 1)
    copies = []
    for step in range(1, n):
        copy = pltpu.make_async_remote_copy(
            src_ref=mine_ref,
            dst_ref=slots.at[step - 1],
            send_sem=send_sem.at[step - 1],
            recv_sem=recv_sem.at[step - 1],
            device_id={"row": lax.rem(me + step, n)},
            device_id_type=pl.DeviceIdType.MESH,
        )
        copy.start()
        copies.append(copy)
    value = mine_ref[...]
    for step in range(1, n):
        copies[step - 1].wait()
        value = jnp.maximum(value, slots[step - 1])
    out_ref[...] = value


def best_of_row(n, value):
    return pl.pallas_call(
        functools.partial(best_kernel, n),
        out_shape=jax.ShapeDtypeStruct(value.shape, value.dtype),
        in_specs=[pl.BlockSpec(memory_space=pltpu.VMEM)],
        out_specs=pl.BlockSpec(memory_space=pltpu.VMEM),
        scratch_shapes=[
            pltpu.VMEM((n - 1,) + value.shape, value.dtype),
            pltpu.SemaphoreType.DMA((n - 1,)),
            pltpu.SemaphoreType.DMA((n - 1,)),
        ],
        compiler_params=pltpu.CompilerParams(collective_id=0, has_side_effects=True),
        name="best_of_row",
    )(value)


def body(n, raw_trace, fir_taps, templ_real, templ_imag, channel_mask, moveout):
    local, windows, length = raw_trace.shape
    samples = length // 2
    band, channels, templates = templ_real.shape
    held = -(-2 * local // 8) * 8
    depth = n * held
    block = math.gcd(windows, 128)
    blocks = windows // block
    bins = FIRST_BIN + np.arange(band)
    lags = np.arange(samples)
    angle = 2.0 * np.pi / samples * (bins[:, None] * lags[None, :] % samples)
    inverse = np.concatenate([np.cos(angle), -np.sin(angle)], axis=0)
    forward = jnp.asarray(inverse.T, jnp.float32)
    inverse = inverse.T.astype(np.float32)
    inverse_high = jnp.asarray(inverse).astype(jnp.bfloat16)
    high_np = np.asarray(inverse.astype(jnp.bfloat16))
    inverse_low = jnp.asarray((inverse - high_np.astype(np.float32)).astype(jnp.bfloat16))
    inverse3 = jnp.concatenate([inverse_high, inverse_high, inverse_low], axis=1)

    vmem = pl.BlockSpec(memory_space=pltpu.VMEM)
    spectra = pl.pallas_call(
        front_kernel,
        grid=(blocks,),
        out_shape=jax.ShapeDtypeStruct((blocks, band * held, block), jnp.bfloat16),
        in_specs=[
            pl.BlockSpec(memory_space=pltpu.SMEM),
            vmem,
            pl.BlockSpec((local, block, length), lambda i: (0, i, 0)),
        ],
        out_specs=pl.BlockSpec((1, band * held, block), lambda i: (i, 0, 0)),
        scratch_shapes=[
            pltpu.VMEM((length, 4 * band), jnp.bfloat16),
            pltpu.VMEM((band * held, block), jnp.float32),
        ],
        compiler_params=pltpu.CompilerParams(vmem_limit_bytes=VMEM_LIMIT),
        name="front",
    )(fir_taps, forward, raw_trace)
    spectra = spectra.reshape(blocks, band, held, block)

    def rows_of(first, second):
        shape = first.shape[:-2] + (n, local, templates)
        joined = jnp.concatenate([first.reshape(shape), second.reshape(shape)], axis=-2)
        if held > 2 * local:
            joined = jnp.pad(joined, [(0, 0)] * (joined.ndim - 2) + [(0, held - 2 * local), (0, 0)])
        return joined.reshape(first.shape[:-2] + (depth, templates))

    x = rows_of(templ_real, templ_imag)
    y = rows_of(templ_imag, -templ_real)
    turn = 2.0 * math.pi / samples
    first_phase = turn * (FIRST_BIN * moveout % samples).astype(jnp.float32)
    step_phase = turn * moveout.astype(jnp.float32)
    weight = channel_mask.astype(jnp.float32)
    tables = [
        weight * jnp.cos(first_phase),
        weight * jnp.sin(first_phase),
        jnp.cos(step_phase),
        jnp.sin(step_phase),
    ]
    tables = [rows_of(table, table) for table in tables]
    count = math.gcd(band, 4)
    pitch = 2 * band + 8
    anywhere = pl.BlockSpec(memory_space=pl.ANY)
    highest, energy, square, _ = pl.pallas_call(
        functools.partial(scan_kernel, n, pitch, count),
        out_shape=(
            jax.ShapeDtypeStruct((templates, windows), jnp.float32),
            jax.ShapeDtypeStruct((blocks, 1, block), jnp.float32),
            jax.ShapeDtypeStruct((1, templates), jnp.float32),
            jax.ShapeDtypeStruct((blocks, band, depth, block), jnp.bfloat16),
        ),
        in_specs=[vmem] * 7 + [anywhere],
        out_specs=(vmem, vmem, vmem, anywhere),
        scratch_shapes=[
            pltpu.VMEM((band, 2 * templates, depth), jnp.bfloat16),
            pltpu.VMEM((depth, templates), jnp.float32),
            pltpu.VMEM((depth, templates), jnp.float32),
            pltpu.VMEM((band, depth, block), jnp.bfloat16),
            pltpu.VMEM((templates * pitch, block), jnp.float32),
            pltpu.VMEM((8, max(block, templates)), jnp.float32),
            pltpu.SemaphoreType.DMA((3 * n, blocks)),
            pltpu.SemaphoreType.DMA((blocks, n)),
            pltpu.SemaphoreType.DMA((blocks,)),
            pltpu.SemaphoreType.DMA((band // count,)),
        ],
        compiler_params=pltpu.CompilerParams(
            collective_id=1, has_side_effects=True, vmem_limit_bytes=VMEM_LIMIT
        ),
        name="gather_scan",
    )(x, y, *tables, inverse3, spectra)
    data_norm = jnp.sqrt(energy.reshape(1, windows) + epsilon)
    templ_norm = jnp.sqrt(square + epsilon).reshape(templates, 1)
    scale = math.sqrt(2.0 * channels * band)
    peak = highest * scale / (templ_norm * data_norm)
    best = best_of_row(n, jnp.max(peak, axis=0).reshape(blocks, block))
    return (peak, best.reshape(windows))


def solution(mesh):
    in_specs = (
        P("row", "parts", None),
        P(),
        P(None, None, "row"),
        P(None, None, "row"),
        P(None, "row"),
        P(None, "row"),
    )
    out_specs = (P("row", "parts"), P("parts"))
    return jax.shard_map(
        functools.partial(body, mesh.shape["row"]),
        mesh=mesh,
        in_specs=in_specs,
        out_specs=out_specs,
        check_vma=False,
    )
```
